32 devices in a mesh: band: 4 (over y, core), lev: 8 (over z, x).
Axes of the slice: x: 2, y: 2, z: 4, core: 2. Of those that a mesh axis runs over, the one named last changes fastest.
Arguments:
- azimuthal_coeffs: bfloat16 [2560, 64, 64], P('band', 'lev'), may hold values from -6 to 6
- polynomial_tables: bfloat16 [32, 2, 448, 1280], P(('band', 'lev')), may hold values from -0.15625 to 0.15625
- gauss_masses: float32 [1280], replicated, may hold values from 0.3 to 1.5
- circle_samples: int32 [1280], replicated, may hold values from 20 to 152, as said below
- table_lookup: int32 [32], replicated, may hold values from 0 to 31, each once
- eigen_basis: float32 [16, 16], replicated, may hold values from -1.5 to 1.5
- basis_mapping: float32 [16, 16], replicated, may hold values from -1.5 to 1.5
- eigen_constants: float32 [16], replicated, may hold values from 0.5 to 2
- hydrostatic_matrix: float32 [16, 16], replicated, may hold values from -1.5 to 1.5
- thermal_response: float32 [16, 16], replicated, may hold values from -1.5 to 1.5
Outputs:
- advanced: bfloat16 [2560, 64, 64], P('band', 'lev')
The draws below stay inside these ranges and needn't reach their ends.
Inputs may be any that keep to these rules, and one draw needn't show every extreme that they name: circle_samples[j] is 20 + 4 * floor(j * 32 / 1280) plus 0, 4 or 8; row 0 holds 20 and row 1279 the largest value. table_lookup is a permutation of 0 .. 31.
All inputs are finite; a program needn't handle non-finite values.
Results may differ from the reference program's by a relative error of at most 0.0041.
The reference program's roundings to bfloat16 on the way count: a program that leaves them out, or rounds other values in their place, can miss the bound.
Values may be sent and summed in bfloat16 or wider, within the bound.
No kernel may reach another device: no remote copies, remote signals or barrier semaphores. Data moves between devices by JAX's collectives and lax.ppermute only.
A program may use at most 64 MiB of HBM per device.

```python
import math
import jax
import jax.numpy as jnp
from jax import lax

LATH = 1280
TRUNC = 1280
FIELDS = 4
COLUMN_HEIGHTS = 16
M = 32
LAT = 2560
NTH = 448
K = 64


def draw_circle_samples(key, part):
    row_index = jnp.arange(LATH, dtype=jnp.int32)
    extra = jax.random.randint(key, (LATH,), 0, 3, dtype=jnp.int32)
    extra = jnp.where(row_index == 0, 0, jnp.where(row_index == LATH - 1, 2, extra))
    return (20 + 4 * (row_index * M // LATH) + 4 * extra).astype(jnp.int32)


def level_of(own_key, extent, shards, low, high):
    loudness = 1.0
    for position, shards_of in shards:
        steps = jax.random.uniform(jax.random.fold_in(jax.random.fold_in(own_key, 6), position), (shards_of,), jnp.float32, low / len(shards), high / len(shards))
        loudness = loudness * jnp.repeat(jnp.exp(steps), extent[position] // shards_of).reshape((-1,) + (1,) * (len(extent) - 1 - position))
    return loudness


def noise(key, extent, width, most, split=(), held_as=jnp.bfloat16):
    array = jax.random.normal(key, extent, jnp.float32) * width
    if len(split) > 0:
        array = level_of(key, extent, split, -0.22, 0.18) * array
    return jnp.clip(array, min=-most, max=most).astype(held_as)


def setup_inputs(seed: int = 0) -> dict:
    key_of = jax.random.split(jax.random.key(seed), 11)
    return {
        "azimuthal_coeffs": noise(key_of[0], (LAT, K, 2 * M), 1.0, 6.0, ((0, 4), (1, 8))),
        "polynomial_tables": noise(key_of[1], (M, 2, NTH, LATH), LATH ** -0.5, 0.15625, ((0, 32),)),
        "gauss_masses": jnp.clip(jnp.exp(jax.random.uniform(key_of[2], (LATH,), jnp.float32, math.log(0.3), math.log(1.5))), 0.3, 1.5),
        "circle_samples": draw_circle_samples(jax.random.fold_in(key_of[10], 71), 0),
        "table_lookup": jax.random.permutation(key_of[4], M).astype(jnp.int32),
        "eigen_basis": noise(key_of[5], (COLUMN_HEIGHTS, COLUMN_HEIGHTS), COLUMN_HEIGHTS ** -0.5, 1.5, (), jnp.float32),
        "basis_mapping": noise(key_of[6], (COLUMN_HEIGHTS, COLUMN_HEIGHTS), COLUMN_HEIGHTS ** -0.5, 1.5, (), jnp.float32),
        "eigen_constants": jnp.clip(jnp.exp(jax.random.uniform(key_of[7], (COLUMN_HEIGHTS,), jnp.float32, math.log(0.5), math.log(2.0))), 0.5, 2.0),
        "hydrostatic_matrix": noise(key_of[8], (COLUMN_HEIGHTS, COLUMN_HEIGHTS), COLUMN_HEIGHTS ** -0.5, 1.5, (), jnp.float32),
        "thermal_response": noise(key_of[9], (COLUMN_HEIGHTS, COLUMN_HEIGHTS), COLUMN_HEIGHTS ** -0.5, 1.5, (), jnp.float32),
    }


TRUNCATION_LIMIT = lax.Precision.HIGHEST
STIFFNESS = 8.0
DIFFUSION = 4.0


def harmonic_advance(harmonic_current, total_order, eigen_basis, basis_mapping, eigen_constants, hydrostatic_matrix, thermal_response):
    scaled = total_order * (total_order + 1.0) / (TRUNC * (TRUNC + 1.0))
    implicit_weighting = STIFFNESS * scaled
    rotational_curl = harmonic_current[:, 0]
    dilatation_current = harmonic_current[:, 1]
    thermal_current = harmonic_current[:, 2]
    moisture = harmonic_current[:, 3]
    hyper_viscosity = 1.0 / (1.0 + DIFFUSION * scaled * scaled)
    explicit_righthand = dilatation_current + implicit_weighting[:, None, None] * jnp.einsum("li,eic->elc", hydrostatic_matrix, thermal_current, precision=TRUNCATION_LIMIT)
    projected = jnp.einsum("li,eic->elc", basis_mapping, explicit_righthand, precision=TRUNCATION_LIMIT)
    projected = projected / (1.0 + implicit_weighting[:, None, None] * eigen_constants[None, :, None])
    dilatation_future = jnp.einsum("li,eic->elc", eigen_basis, projected, precision=TRUNCATION_LIMIT)
    thermal_future = thermal_current - jnp.einsum("li,eic->elc", thermal_response, dilatation_future, precision=TRUNCATION_LIMIT)
    return jnp.stack([rotational_curl * hyper_viscosity[:, None, None], dilatation_future, thermal_future, moisture * hyper_viscosity[:, None, None]], axis=1)


def analyse_wave(column, zonal_order, operator_array, gauss_masses, circle_samples):
    half_rows = operator_array.shape[2]
    live_mask = (2 * zonal_order < circle_samples).astype(jnp.float32)
    north = column[:half_rows].astype(jnp.float32)
    south = jnp.flip(column[half_rows:], axis=0).astype(jnp.float32)
    weight_col = (gauss_masses * live_mask)[:, None]
    even_part = ((north + south) * weight_col).astype(jnp.bfloat16)
    odd_part = ((north - south) * weight_col).astype(jnp.bfloat16)
    spec_even = jnp.dot(operator_array[0], even_part, preferred_element_type=jnp.float32)
    spec_odd = jnp.dot(operator_array[1], odd_part, preferred_element_type=jnp.float32)
    return jnp.stack([spec_even, spec_odd], axis=0)


def complete_harmonic(harmonic_coeffs, zonal_order, operator_array, circle_samples, eigen_basis, basis_mapping, eigen_constants, hydrostatic_matrix, thermal_response):
    pair_rows = harmonic_coeffs.shape[1]
    col_count = harmonic_coeffs.shape[2]
    offsets = jnp.arange(pair_rows, dtype=jnp.int32) * 2 + zonal_order
    keep_even = (offsets < TRUNC).astype(jnp.float32)[:, None]
    keep_odd = (offsets + 1 < TRUNC).astype(jnp.float32)[:, None]
    harmonic_current = jnp.concatenate([harmonic_coeffs[0] * keep_even, harmonic_coeffs[1] * keep_odd], axis=0)
    total_order = jnp.concatenate([offsets, offsets + 1]).astype(jnp.float32)
    arranged = harmonic_current.reshape(2 * pair_rows, FIELDS, col_count // (2 * FIELDS), 2)
    refreshed = harmonic_advance(arranged, total_order, eigen_basis, basis_mapping, eigen_constants, hydrostatic_matrix, thermal_response)
    refreshed = refreshed.reshape(2 * pair_rows, col_count).astype(jnp.bfloat16)
    contract = (((0,), (0,)), ((), ()))
    even_sum = lax.dot_general(operator_array[0], refreshed[:pair_rows], contract, preferred_element_type=jnp.float32)
    odd_sum = lax.dot_general(operator_array[1], refreshed[pair_rows:], contract, preferred_element_type=jnp.float32)
    live_col = (2 * zonal_order < circle_samples).astype(jnp.float32)[:, None]
    north_out = (even_sum + odd_sum) * live_col
    south_out = (even_sum - odd_sum) * live_col
    return jnp.concatenate([north_out, jnp.flip(south_out, axis=0)], axis=0).astype(jnp.bfloat16)


def reference(azimuthal_coeffs, polynomial_tables, gauss_masses, circle_samples, table_lookup, eigen_basis, basis_mapping, eigen_constants, hydrostatic_matrix, thermal_response):
    lat_count = azimuthal_coeffs.shape[0]
    col_count = azimuthal_coeffs.shape[1]
    wave_count = azimuthal_coeffs.shape[2] // 2
    by_wave = jnp.transpose(azimuthal_coeffs.reshape(lat_count, col_count, wave_count, 2), (2, 0, 1, 3))
    by_wave = by_wave.reshape(wave_count, lat_count, 2 * col_count)

    def one_wave(packed):
        column, zonal_order, slot = packed
        operator_array = lax.dynamic_index_in_dim(polynomial_tables, slot, 0, keepdims=False)
        harmonic_coeffs = analyse_wave(column, zonal_order, operator_array, gauss_masses, circle_samples)
        return complete_harmonic(harmonic_coeffs, zonal_order, operator_array, circle_samples, eigen_basis, basis_mapping, eigen_constants, hydrostatic_matrix, thermal_response)

    result = lax.map(one_wave, (by_wave, jnp.arange(wave_count, dtype=jnp.int32), table_lookup.astype(jnp.int32)))
    result = jnp.transpose(result.reshape(wave_count, lat_count, col_count, 2), (1, 2, 0, 3))
    return result.reshape(lat_count, col_count, 2 * wave_count)
```

```python
import functools

import jax
import jax.numpy as jnp
from jax import lax
from jax.experimental import pallas as pl
from jax.experimental.pallas import tpu as pltpu
from jax.sharding import PartitionSpec as P

TRUNC = 1280
FIELDS = 4
STIFFNESS = 8.0
DIFFUSION = 4.0
LANES = 128
HIGHEST = lax.Precision.HIGHEST
F32 = jnp.float32
BF16 = jnp.bfloat16
I32 = jnp.int32
VMEM_BYTES = 24 * 2**20


def iota(shape, dim):
    return lax.broadcasted_iota(I32, shape, dim)


def dot32(a, b):
    return jnp.dot(a, b, precision=HIGHEST, preferred_element_type=F32)


def owner_rows(lookup, width, columns):
    waves = lookup.shape[1]
    row = iota((1, columns), 1)
    level, place = lax.div(row, width), lax.rem(row, width)
    pick = (iota((waves, columns), 0) == lax.div(lax.rem(iota((waves, columns), 1), width), 2)).astype(F32)
    owner = dot32(lookup.astype(F32), pick).astype(I32)
    per_owner = 2 * (columns // width)
    return owner * per_owner + level * 2 + lax.rem(place, 2)


def send_kernel(width, block, lookup_ref, x_ref, out_ref):
    columns = x_ref.shape[0]
    target = owner_rows(lookup_ref[...], width, columns)
    row = iota((block, columns), 0) + pl.program_id(0) * block
    pick = (row == target).astype(F32).astype(BF16)
    out_ref[...] = jnp.dot(pick, x_ref[...], preferred_element_type=F32).astype(BF16)


def back_kernel(width, block, lookup_ref, x_ref, out_ref):
    columns = x_ref.shape[0]
    waves = lookup_ref.shape[1]
    row = iota((block, 1), 0) + pl.program_id(0) * block
    level, place = lax.div(row, width), lax.rem(row, width)
    mine = iota((block, waves), 1) == lax.div(lax.rem(iota((block, waves), 0) + pl.program_id(0) * block, width), 2)
    owner = jnp.sum(jnp.where(mine, lookup_ref[...].astype(F32), 0.0), axis=1, keepdims=True).astype(I32)
    target = owner * (2 * (columns // width)) + level * 2 + lax.rem(place, 2)
    pick = (iota((block, columns), 1) == target).astype(F32).astype(BF16)
    out_ref[...] = jnp.dot(pick, x_ref[...], preferred_element_type=F32).astype(BF16)


def pair_up(small):
    n = small.shape[0]
    left = (lax.div(iota((2 * n, n), 0), 2) == iota((2 * n, n), 1)).astype(F32)
    right = (iota((n, 2 * n), 0) == lax.div(iota((n, 2 * n), 1), 2)).astype(F32)
    same = lax.rem(iota((2 * n, 2 * n), 0), 2) == lax.rem(iota((2 * n, 2 * n), 1), 2)
    return jnp.where(same, dot32(dot32(left, small), right), 0.0)


def prep_kernel(
    lev_count,
    lookup_ref,
    masses_ref,
    samples_ref,
    eigen_basis_ref,
    basis_mapping_ref,
    eigen_constants_ref,
    hydrostatic_ref,
    thermal_ref,
    rows_ref,
    first_ref,
    second_ref,
    degree_ref,
    scale_ref,
):
    waves = lookup_ref.shape[1]
    me = lax.axis_index("band") * lev_count + lax.axis_index("lev")
    wave = jnp.sum(
        jnp.where(lookup_ref[...] == me, iota((1, waves), 1), 0).astype(F32), axis=1, keepdims=True
    ).astype(I32)
    live = (2 * wave < samples_ref[...]).astype(F32)
    rows_ref[0:1, :] = live
    rows_ref[1:2, :] = masses_ref[...] * live
    n = 2 * eigen_basis_ref.shape[0]
    mapping = pair_up(basis_mapping_ref[...])
    basis = pair_up(eigen_basis_ref[...])
    first_ref[...] = jnp.zeros(first_ref.shape, F32)
    first_ref[0:n, 0:n] = mapping
    first_ref[n : 2 * n, n : 2 * n] = dot32(mapping, pair_up(hydrostatic_ref[...]))
    second_ref[0:n, :] = basis
    second_ref[n : 2 * n, :] = dot32(pair_up(thermal_ref[...]), basis)
    half = n // 2
    spread = lax.div(iota((n, half), 0), 2) == iota((n, half), 1)
    constants = jnp.sum(jnp.where(spread, eigen_constants_ref[...], 0.0), axis=1, keepdims=True)
    nth = degree_ref.shape[2]
    for parity in range(2):
        degree = iota((1, nth), 1) * 2 + wave + parity
        keep = (degree < TRUNC).astype(F32)
        order = degree.astype(F32)
        scaled = order * (order + 1.0) / (TRUNC * (TRUNC + 1.0))
        weight = STIFFNESS * scaled
        degree_ref[parity, 0:1, :] = keep
        degree_ref[parity, 1:2, :] = weight
        degree_ref[parity, 2:3, :] = keep / (1.0 + DIFFUSION * scaled * scaled)
        scale_ref[parity] = 1.0 + weight * constants


def step_kernel(z_ref, table_ref, rows_ref, first_ref, second_ref, degree_ref, scale_ref, out_ref, even_ref, odd_ref):
    bands, columns, lats = z_ref.shape
    per = lats // LANES
    half = bands * per // 2
    quarter = columns // FIELDS
    turn = (iota((LANES, LANES), 0) + iota((LANES, LANES), 1) == LANES - 1).astype(F32).astype(BF16)

    def place(i):
        return i // per, pl.ds((i % per) * LANES, LANES)

    for i in range(half):
        b, lanes = place(i)
        north = z_ref[b, :, lanes].astype(F32)
        b, lanes = place(2 * half - 1 - i)
        south = jnp.dot(z_ref[b, :, lanes], turn, preferred_element_type=F32)
        here = pl.ds(i * LANES, LANES)
        weight = rows_ref[1:2, here]
        even_ref[:, here] = ((north + south) * weight).astype(BF16)
        odd_ref[:, here] = ((north - south) * weight).astype(BF16)

    fresh = []
    for parity, side in ((0, even_ref), (1, odd_ref)):
        spec = lax.dot_general(side[...], table_ref[parity], (((1,), (1,)), ((), ())), preferred_element_type=F32)
        keep = degree_ref[parity, 0:1, :]
        weight = degree_ref[parity, 1:2, :]
        damp = degree_ref[parity, 2:3, :]
        middle = spec[quarter : 3 * quarter] * keep
        mixed = dot32(first_ref[...], middle)
        projected = (mixed[:quarter] + weight * mixed[quarter:]) / scale_ref[parity]
        after = dot32(second_ref[...], projected)
        fresh.append(
            jnp.concatenate(
                [
                    spec[:quarter] * damp,
                    after[:quarter],
                    middle[quarter:] - after[quarter:],
                    spec[3 * quarter :] * damp,
                ],
                axis=0,
            ).astype(BF16)
        )
    even = jnp.dot(fresh[0], table_ref[0], preferred_element_type=F32)
    odd = jnp.dot(fresh[1], table_ref[1], preferred_element_type=F32)
    for i in range(half):
        here = slice(i * LANES, (i + 1) * LANES)
        live = rows_ref[0:1, here]
        b, lanes = place(i)
        out_ref[b, :, lanes] = ((even[:, here] + odd[:, here]) * live).astype(BF16)
        lower = ((even[:, here] - odd[:, here]) * live).astype(BF16)
        b, lanes = place(2 * half - 1 - i)
        out_ref[b, :, lanes] = jnp.dot(lower, turn, preferred_element_type=F32).astype(BF16)


def whole(shape):
    return pl.BlockSpec(shape, lambda *_: (0,) * len(shape))


def permute(kernel, name, lookup, x, width):
    columns, lats = x.shape
    block = min(columns, 512)
    return pl.pallas_call(
        functools.partial(kernel, width, block),
        name=name,
        grid=(columns // block,),
        in_specs=[whole(lookup.shape), whole(x.shape)],
        out_specs=pl.BlockSpec((block, lats), lambda i: (i, 0)),
        out_shape=jax.ShapeDtypeStruct(x.shape, BF16),
        compiler_params=pltpu.CompilerParams(vmem_limit_bytes=VMEM_BYTES),
        cost_estimate=pl.CostEstimate(flops=2 * columns * columns * lats, bytes_accessed=4 * columns * lats, transcendentals=0),
    )(lookup, x)


def per_device(
    azimuthal_coeffs,
    polynomial_tables,
    gauss_masses,
    circle_samples,
    table_lookup,
    eigen_basis,
    basis_mapping,
    eigen_constants,
    hydrostatic_matrix,
    thermal_response,
):
    lats, levels, width = azimuthal_coeffs.shape
    waves = width // 2
    bands = lax.axis_size("band")
    levs = lax.axis_size("lev")
    devices = bands * levs
    columns = 2 * levels * levs
    table = polynomial_tables[0]
    nth, lath = table.shape[1:]
    lookup = table_lookup.reshape(1, waves)

    x = jnp.transpose(azimuthal_coeffs, (1, 2, 0)).reshape(levels * width, lats)
    sent = permute(send_kernel, "send", lookup, x, width).reshape(devices, 2 * levels, lats)
    got = lax.all_to_all(sent, ("band", "lev"), 0, 0, tiled=True).reshape(bands, columns, lats)

    n = 2 * eigen_basis.shape[0]
    small = [
        lookup,
        gauss_masses.reshape(1, lath),
        circle_samples.reshape(1, lath),
        eigen_basis,
        basis_mapping,
        eigen_constants.reshape(1, n // 2),
        hydrostatic_matrix,
        thermal_response,
    ]
    made = [(2, lath), (2 * n, 2 * n), (2 * n, n), (2, 3, nth), (2, n, nth)]
    prepared = pl.pallas_call(
        functools.partial(prep_kernel, levs),
        name="prep",
        out_shape=[jax.ShapeDtypeStruct(shape, F32) for shape in made],
        compiler_params=pltpu.CompilerParams(vmem_limit_bytes=VMEM_BYTES),
        cost_estimate=pl.CostEstimate(flops=10**8, bytes_accessed=10**6, transcendentals=0),
    )(*small)

    aligned = lats % LANES == 0 and bands % 2 == 0
    if not aligned:
        got = jnp.transpose(got.reshape(2, bands // 2, columns, lats), (0, 2, 1, 3)).reshape(2, columns, lath)
    result = pl.pallas_call(
        step_kernel,
        name="step",
        out_shape=jax.ShapeDtypeStruct(got.shape, BF16),
        scratch_shapes=[pltpu.VMEM((columns, lath), BF16)] * 2,
        compiler_params=pltpu.CompilerParams(vmem_limit_bytes=VMEM_BYTES),
        cost_estimate=pl.CostEstimate(
            flops=8 * columns * nth * lath, bytes_accessed=4 * nth * lath + 8 * columns * lath, transcendentals=0
        ),
    )(got, table, *prepared)
    if not aligned:
        result = jnp.transpose(result.reshape(2, columns, bands // 2, lats), (0, 2, 1, 3))
    result = result.reshape(devices, 2 * levels, lats)

    returned = lax.all_to_all(result, ("band", "lev"), 0, 0, tiled=True).reshape(levels * width, lats)
    out = permute(back_kernel, "back", lookup, returned, width)
    return jnp.transpose(out.reshape(levels, width, lats), (2, 0, 1))


def solution(mesh):
    placed = (P("band", "lev", None), P(("band", "lev"), None, None, None)) + (P(),) * 8
    return jax.shard_map(
        per_device, mesh=mesh, in_specs=placed, out_specs=P("band", "lev", None), check_vma=False
    )
```

```python
import functools

import jax
import jax.numpy as jnp
from jax import lax
from jax.experimental import pallas as pl
from jax.experimental.pallas import tpu as pltpu
from jax.sharding import PartitionSpec as P

TRUNC = 1280
FIELDS = 4
STIFFNESS = 8.0
DIFFUSION = 4.0
LANES = 128
SUBLANES = 8
HIGHEST = lax.Precision.HIGHEST
F32 = jnp.float32
BF16 = jnp.bfloat16
I32 = jnp.int32
VMEM_BYTES = 24 * 2**20


def iota(shape, dim):
    return lax.broadcasted_iota(I32, shape, dim)


def dot32(a, b):
    return jnp.dot(a, b, precision=HIGHEST, preferred_element_type=F32)


def halves(x):
    high = x.astype(BF16)
    return high, (x - high.astype(F32)).astype(BF16)


def send_kernel(width, lookup_hbm, x_hbm, out_ref, lookup, held, wide, small_sem, sems):
    columns, lats = x_hbm.shape
    levels, waves, tiles = columns // width, width // 2, lats // LANES
    copies = [
        pltpu.make_async_copy(x_hbm.at[:, pl.ds(t * LANES, LANES)], held.at[t], sems.at[t]) for t in range(tiles)
    ]
    small = pltpu.make_async_copy(lookup_hbm, lookup, small_sem)
    small.start()
    for copy in copies:
        copy.start()
    small.wait()
    for t in range(tiles):
        copies[t].wait()
        wide[t] = held[t].astype(F32)
        for m in range(waves):
            parts = [wide[t, pl.ds(2 * m + c, levels, stride=width), :] for c in range(2)]
            out_ref[lookup[m], :, pl.ds(t * LANES, LANES)] = jnp.concatenate(parts, axis=0).astype(BF16)


def back_kernel(width, lookup_hbm, x_ref, out_hbm, lookup, held, wide, small_sem, sems):
    columns, lats = out_hbm.shape
    levels, waves, tiles = columns // width, width // 2, lats // LANES
    small = pltpu.make_async_copy(lookup_hbm, lookup, small_sem)
    small.start()
    small.wait()
    copies = []
    for t in range(tiles):
        for m in range(waves):
            block = x_ref[lookup[m], :, pl.ds(t * LANES, LANES)].astype(F32)
            for c in range(2):
                wide[t, pl.ds(2 * m + c, levels, stride=width), :] = block[c * levels : (c + 1) * levels]
        held[t] = wide[t].astype(BF16)
        copy = pltpu.make_async_copy(held.at[t], out_hbm.at[:, pl.ds(t * LANES, LANES)], sems.at[t])
        copy.start()
        copies.append(copy)
    for copy in copies:
        copy.wait()


def owner_rows(lookup, width, columns):
    waves = lookup.shape[1]
    levels = columns // width
    row = iota((1, columns), 1)
    pick = (iota((waves, columns), 0) == lax.div(lax.rem(iota((waves, columns), 1), width), 2)).astype(F32)
    owner = dot32(lookup.astype(F32), pick).astype(I32)
    return owner * (2 * levels) + lax.rem(row, 2) * levels + lax.div(row, width)


def send_by_matmul(width, block, lookup_ref, x_ref, out_ref):
    columns = x_ref.shape[0]
    target = owner_rows(lookup_ref[...], width, columns)
    row = iota((block, columns), 0) + pl.program_id(0) * block
    pick = (row == target).astype(F32).astype(BF16)
    out_ref[...] = jnp.dot(pick, x_ref[...], preferred_element_type=F32).astype(BF16)


def back_by_matmul(width, block, lookup_ref, x_ref, out_ref):
    columns = x_ref.shape[0]
    waves = lookup_ref.shape[1]
    levels = columns // width
    row = iota((block, 1), 0) + pl.program_id(0) * block
    mine = iota((block, waves), 1) == lax.div(lax.rem(iota((block, waves), 0) + pl.program_id(0) * block, width), 2)
    owner = jnp.sum(jnp.where(mine, lookup_ref[...].astype(F32), 0.0), axis=1, keepdims=True).astype(I32)
    target = owner * (2 * levels) + lax.rem(row, 2) * levels + lax.div(row, width)
    pick = (iota((block, columns), 1) == target).astype(F32).astype(BF16)
    out_ref[...] = jnp.dot(pick, x_ref[...], preferred_element_type=F32).astype(BF16)


def level_of(row, levels):
    return lax.div(row, 2 * levels) * levels + lax.rem(row, levels)


def part_of(row, levels):
    return lax.rem(lax.div(row, levels), 2)


def pair_up(small, levels):
    n = small.shape[0]
    left = (level_of(iota((2 * n, n), 0), levels) == iota((2 * n, n), 1)).astype(F32)
    right = (iota((n, 2 * n), 0) == level_of(iota((n, 2 * n), 1), levels)).astype(F32)
    square = (2 * n, 2 * n)
    same = part_of(iota(square, 0), levels) == part_of(iota(square, 1), levels)
    return jnp.where(same, dot32(dot32(left, small), right), 0.0)


def mix(matrix, values):
    high, low = halves(matrix)
    top, rest = halves(values)
    return jnp.dot(
        jnp.concatenate([high, high, low], axis=1),
        jnp.concatenate([top, rest, top], axis=0),
        preferred_element_type=F32,
    )


def step_kernel(
    lev_count,
    levels,
    z_ref,
    table_ref,
    lookup_ref,
    masses_ref,
    samples_ref,
    eigen_basis_ref,
    basis_mapping_ref,
    eigen_constants_ref,
    hydrostatic_ref,
    thermal_ref,
    out_ref,
    even_ref,
    odd_ref,
):
    bands, columns, lats = z_ref.shape
    per = lats // LANES
    half = bands * per // 2
    quarter = columns // FIELDS
    nth = table_ref.shape[1]
    turn = (iota((LANES, LANES), 0) + iota((LANES, LANES), 1) == LANES - 1).astype(F32).astype(BF16)

    waves = lookup_ref.shape[1]
    me = lax.axis_index("band") * lev_count + lax.axis_index("lev")
    wave = jnp.sum(
        jnp.where(lookup_ref[...] == me, iota((1, waves), 1), 0).astype(F32), axis=1, keepdims=True
    ).astype(I32)
    live = (2 * wave < samples_ref[...]).astype(F32)
    weights = masses_ref[...] * live

    def place(i):
        return i // per, pl.ds((i % per) * LANES, LANES)

    for i in range(half):
        b, lanes = place(i)
        north = z_ref[b, :, lanes].astype(F32)
        b, lanes = place(2 * half - 1 - i)
        south = jnp.dot(z_ref[b, :, lanes], turn, preferred_element_type=F32)
        here = slice(i * LANES, (i + 1) * LANES)
        weight = weights[:, here]
        even_ref[:, here] = ((north + south) * weight).astype(BF16)
        odd_ref[:, here] = ((north - south) * weight).astype(BF16)

    mapping = pair_up(basis_mapping_ref[...], levels)
    basis = pair_up(eigen_basis_ref[...], levels)
    from_heat = dot32(mapping, pair_up(hydrostatic_ref[...], levels))
    to_heat = dot32(pair_up(thermal_ref[...], levels), basis)
    nothing = jnp.zeros((quarter, quarter), F32)
    first = jnp.concatenate(
        [jnp.concatenate([mapping, nothing], axis=1), jnp.concatenate([nothing, from_heat], axis=1)], axis=0
    )
    second = jnp.concatenate([basis, to_heat], axis=0)
    spread = (quarter, quarter // 2)
    chosen = level_of(iota(spread, 0), levels) == iota(spread, 1)
    constants = jnp.sum(jnp.where(chosen, eigen_constants_ref[...], 0.0), axis=1, keepdims=True)

    fresh = []
    for parity, side in ((0, even_ref), (1, odd_ref)):
        spec = lax.dot_general(side[...], table_ref[parity], (((1,), (1,)), ((), ())), preferred_element_type=F32)
        degree = iota((1, nth), 1) * 2 + wave + parity
        keep = (degree < TRUNC).astype(F32)
        order = degree.astype(F32)
        scaled = order * (order + 1.0) / (TRUNC * (TRUNC + 1.0))
        weight = STIFFNESS * scaled
        damp = keep / (1.0 + DIFFUSION * scaled * scaled)
        middle = spec[quarter : 3 * quarter] * keep
        mixed = mix(first, middle)
        projected = (mixed[:quarter] + weight * mixed[quarter:]) / (1.0 + weight * constants)
        after = mix(second, projected)
        fresh.append(
            jnp.concatenate(
                [
                    spec[:quarter] * damp,
                    after[:quarter],
                    middle[quarter:] - after[quarter:],
                    spec[3 * quarter :] * damp,
                ],
                axis=0,
            ).astype(BF16)
        )
    even = jnp.dot(fresh[0], table_ref[0], preferred_element_type=F32)
    odd = jnp.dot(fresh[1], table_ref[1], preferred_element_type=F32)
    for i in range(half):
        here = slice(i * LANES, (i + 1) * LANES)
        b, lanes = place(i)
        out_ref[b, :, lanes] = ((even[:, here] + odd[:, here]) * live[:, here]).astype(BF16)
        lower = ((even[:, here] - odd[:, here]) * live[:, here]).astype(BF16)
        b, lanes = place(2 * half - 1 - i)
        out_ref[b, :, lanes] = jnp.dot(lower, turn, preferred_element_type=F32).astype(BF16)


def whole(shape):
    return pl.BlockSpec(shape, lambda *_: (0,) * len(shape))


def by_matmul(kernel, name, lookup, x, width):
    columns, lats = x.shape
    block = min(columns, 512)
    return pl.pallas_call(
        functools.partial(kernel, width, block),
        name=name,
        grid=(columns // block,),
        in_specs=[whole(lookup.shape), whole(x.shape)],
        out_specs=pl.BlockSpec((block, lats), lambda i: (i, 0)),
        out_shape=jax.ShapeDtypeStruct(x.shape, BF16),
        compiler_params=pltpu.CompilerParams(vmem_limit_bytes=VMEM_BYTES),
    )(lookup, x)


ANY = pl.BlockSpec(memory_space=pl.ANY)
VMEM = pl.BlockSpec(memory_space=pltpu.VMEM)


def by_rows(kernel, name, lookup, x, out_shape, columns, width, lats, in_spec, out_spec):
    tiles = lats // LANES
    return pl.pallas_call(
        functools.partial(kernel, width),
        name=name,
        in_specs=[ANY, in_spec],
        out_specs=out_spec,
        out_shape=jax.ShapeDtypeStruct(out_shape, BF16),
        scratch_shapes=[
            pltpu.SMEM(lookup.shape, I32),
            pltpu.VMEM((tiles, columns, LANES), BF16),
            pltpu.VMEM((tiles, columns, LANES), F32),
            pltpu.SemaphoreType.DMA,
            pltpu.SemaphoreType.DMA((tiles,)),
        ],
        compiler_params=pltpu.CompilerParams(vmem_limit_bytes=VMEM_BYTES),
    )(lookup, x)


def per_device(
    azimuthal_coeffs,
    polynomial_tables,
    gauss_masses,
    circle_samples,
    table_lookup,
    eigen_basis,
    basis_mapping,
    eigen_constants,
    hydrostatic_matrix,
    thermal_response,
):
    lats, levels, width = azimuthal_coeffs.shape
    waves = width // 2
    bands = lax.axis_size("band")
    levs = lax.axis_size("lev")
    devices = bands * levs
    columns = 2 * levels * levs
    local = levels * width
    table = polynomial_tables[0]
    nth, lath = table.shape[1:]
    lookup = table_lookup.reshape(1, waves)
    aligned = lats % LANES == 0 and bands % 2 == 0
    strided = aligned and levels == SUBLANES and waves <= 64

    x = jnp.transpose(azimuthal_coeffs, (1, 2, 0)).reshape(local, lats)
    blocks = (devices, 2 * levels, lats)
    if strided:
        sent = by_rows(send_kernel, "send", table_lookup, x, blocks, local, width, lats, ANY, VMEM)
    else:
        sent = by_matmul(send_by_matmul, "send", lookup, x, width).reshape(blocks)
    got = lax.all_to_all(sent, ("band", "lev"), 0, 0, tiled=True).reshape(bands, columns, lats)

    if not aligned:
        got = jnp.transpose(got.reshape(2, bands // 2, columns, lats), (0, 2, 1, 3)).reshape(2, columns, lath)
    result = pl.pallas_call(
        functools.partial(step_kernel, levs, levels),
        name="step",
        out_shape=jax.ShapeDtypeStruct(got.shape, BF16),
        scratch_shapes=[pltpu.VMEM((columns, lath), BF16)] * 2,
        compiler_params=pltpu.CompilerParams(vmem_limit_bytes=VMEM_BYTES),
        cost_estimate=pl.CostEstimate(
            flops=8 * columns * nth * lath, bytes_accessed=4 * nth * lath + 8 * columns * lath, transcendentals=0
        ),
    )(
        got,
        table,
        lookup,
        gauss_masses.reshape(1, lath),
        circle_samples.reshape(1, lath),
        eigen_basis,
        basis_mapping,
        eigen_constants.reshape(1, eigen_constants.shape[0]),
        hydrostatic_matrix,
        thermal_response,
    )
    if not aligned:
        result = jnp.transpose(result.reshape(2, columns, bands // 2, lats), (0, 2, 1, 3))

    returned = lax.all_to_all(result.reshape(blocks), ("band", "lev"), 0, 0, tiled=True)
    if strided:
        out = by_rows(back_kernel, "back", table_lookup, returned, (local, lats), local, width, lats, VMEM, ANY)
    else:
        out = by_matmul(back_by_matmul, "back", lookup, returned.reshape(local, lats), width)
    return jnp.transpose(out.reshape(levels, width, lats), (2, 0, 1))


def solution(mesh):
    placed = (P("band", "lev", None), P(("band", "lev"), None, None, None)) + (P(),) * 8
    return jax.shard_map(
        per_device, mesh=mesh, in_specs=placed, out_specs=P("band", "lev", None), check_vma=False
    )
```
